32 devices in a mesh: row: 4 (over z), col: 4 (over x, core), depth: 2 (over y).
Axes of the slice: x: 2, y: 2, z: 4, core: 2. Of those that a mesh axis runs over, the one named last changes fastest.
Arguments:
- left_block: bfloat16 [4, 8192, 512], P(None, ('row', 'depth'), 'col'), may hold values from -6 to 6
- right_block: bfloat16 [512, 2, 16384], P(('row', 'depth'), None, 'col'), may hold values from -0.125 to 0.125
- slice_ids: int32 [4], replicated, may hold values from 0 to 1, as said below
- mode_order: int32 [9], replicated, may hold values from 0 to 8, each once
Outputs:
- contracted: float32 [8192, 16384], P(('row', 'depth'), 'col')
The draws below stay inside these ranges and needn't reach their ends.
Inputs may be any that keep to these rules, and one draw needn't show every extreme that they name: mode_order holds every number of 0 to 8 once. `slice_ids`: each value of the sliced bond is taken by exactly 2 slices.
All inputs are finite; a program needn't handle non-finite values.
Results may differ from the reference program's by a relative error of at most 0.0003.
Values may be sent and summed in bfloat16 or wider, within the bound.
No kernel may reach another device: no remote copies, remote signals or barrier semaphores. Data moves between devices by JAX's collectives and lax.ppermute only.
A program may use at most 128 MiB of HBM per device.

```python
import jax
import jax.numpy as jnp
from jax import lax

BITS = 9
K = 512
N = 16384
CHOICES = 2
SLICES = 4
M = 8192


def draw_slice_ids(key, part):
    order = jax.random.permutation(jax.random.fold_in(key, 17), SLICES)
    return (order % CHOICES).astype(jnp.int32)


def shard_levels(rng, shape, pieces, smallest, top_value):
    factor_of, own = 1.0, jax.random.fold_in(rng, 6)
    for dim, parts in pieces:
        steps = jnp.exp(jax.random.uniform(jax.random.fold_in(own, dim), (parts,), jnp.float32, smallest / len(pieces), top_value / len(pieces)))
        factor_of = factor_of * jnp.repeat(steps, shape[dim] // parts).reshape([-1 if axis == dim else 1 for axis in range(len(shape))])
    return factor_of


def gaussian(rng, shape, scale, bound, pieces=(), held_as=jnp.bfloat16):
    factor_of = shard_levels(rng, shape, pieces, -0.22, 0.18) if pieces else 1.0
    array = jax.random.normal(rng, shape, jnp.float32) * scale * factor_of
    return jnp.minimum(jnp.maximum(array, -bound), bound).astype(held_as)


def setup_inputs(seed: int = 0) -> dict:
    arg_keys = jax.random.split(jax.random.key(seed), 5)
    left_block = gaussian(arg_keys[0], (SLICES, M, K), 1.0, 6.0, ((1, 8), (2, 4)))
    right_block = gaussian(arg_keys[1], (K, CHOICES, N), (SLICES * K) ** -0.5, 0.125, ((0, 8), (2, 4)))
    slice_ids = draw_slice_ids(jax.random.fold_in(arg_keys[4], 71), 0)
    mode_order = jax.random.permutation(arg_keys[3], BITS).astype(jnp.int32)
    return dict(left_block=left_block, right_block=right_block, slice_ids=slice_ids, mode_order=mode_order)


def stored_order(mode_order, columns):
    logical = jnp.arange(columns, dtype=jnp.int32)
    stored = jnp.zeros((columns,), jnp.int32)
    for bit_place in range(mode_order.shape[0]):
        stored = stored + ((logical // (2 ** bit_place)) % 2) * jnp.left_shift(jnp.int32(1), mode_order[bit_place].astype(jnp.int32))
    return stored.astype(jnp.int32)


def reference(left_block, right_block, slice_ids, mode_order):
    ordered = jnp.take(left_block, stored_order(mode_order, left_block.shape[2]), axis=2)
    total = jnp.zeros((left_block.shape[1], right_block.shape[2]), jnp.float32)
    for number in range(left_block.shape[0]):
        partner = lax.dynamic_index_in_dim(right_block, slice_ids[number].astype(jnp.int32), 1, keepdims=False)
        total = total + jnp.dot(ordered[number].astype(jnp.float32), partner.astype(jnp.float32), preferred_element_type=jnp.float32)
    return total
```

```python
import functools

import jax
import jax.numpy as jnp
from jax import lax
from jax.experimental import pallas as pl
from jax.experimental.pallas import tpu as pltpu
from jax.sharding import PartitionSpec as P


CHUNKS = 4
ROW_BLOCK = 256


def stored_order(mode_order, logical):
    stored = jnp.zeros(logical.shape, jnp.int32)
    for bit_place in range(mode_order.shape[0]):
        stored = stored + (logical // 2**bit_place % 2) * jnp.left_shift(
            jnp.int32(1), mode_order[bit_place]
        )
    return stored


def fold_kernel(slices, choices, scalars, stored_ref, *refs):
    sources = len(refs) - 3
    pieces, (high_ref, low_ref, spread) = refs[:sources], refs[sources:]
    width = pieces[0].shape[2]
    columns = stored_ref.shape[1]

    @pl.when(pl.program_id(0) == 0)
    def _():
        stored = stored_ref[0:1, :]
        choice = stored_ref[1:2, :]
        entry = lax.broadcasted_iota(jnp.int32, (width, columns), 0)
        for source in range(sources):
            here = entry + scalars[slices + source] == stored
            for number in range(slices):
                picked = here & (choice == scalars[number])
                spread[pl.ds((source * slices + number) * width, width), :] = jnp.where(
                    picked, 1.0, 0.0
                ).astype(jnp.bfloat16)

    rows = jnp.concatenate(
        [piece[number] for piece in pieces for number in range(slices)], axis=1
    )
    folded = jnp.dot(rows, spread[...], preferred_element_type=jnp.float32)
    high = folded.astype(jnp.bfloat16)
    high_ref[...] = high
    low_ref[...] = (folded - high.astype(jnp.float32)).astype(jnp.bfloat16)


def fold(pieces, stored, choice, slice_ids, bases):
    slices, rows, width = pieces[0].shape
    columns = stored.shape[0]
    block = min(ROW_BLOCK, rows)
    scalars = jnp.concatenate([slice_ids, bases])
    table = jnp.stack([stored, choice])
    out = jax.ShapeDtypeStruct((rows, columns), jnp.bfloat16)
    spread_rows = len(pieces) * slices * width
    return pl.pallas_call(
        functools.partial(fold_kernel, slices, None),
        out_shape=(out, out),
        grid_spec=pltpu.PrefetchScalarGridSpec(
            num_scalar_prefetch=1,
            grid=(rows // block,),
            in_specs=[pl.BlockSpec((2, columns), lambda i, s: (0, 0))]
            + [pl.BlockSpec((slices, block, width), lambda i, s: (0, i, 0)) for _ in pieces],
            out_specs=[pl.BlockSpec((block, columns), lambda i, s: (i, 0))] * 2,
            scratch_shapes=[pltpu.VMEM((spread_rows, columns), jnp.bfloat16)],
        ),
        cost_estimate=pl.CostEstimate(
            flops=2 * rows * columns * spread_rows,
            bytes_accessed=2 * rows * (spread_rows + 2 * columns),
            transcendentals=0,
        ),
        name="fold",
    )(scalars, table, *pieces)


def product_kernel(kinds, which, high_ref, low_ref, *refs):
    held, arrived = refs[-2], refs[-1]
    out_ref = refs[-3]
    slots = len(kinds)
    rows = held.shape[0] // slots

    def copy(ref, slot):
        return pltpu.make_async_copy(ref, held.at[pl.ds(slot * rows, rows), :], arrived.at[slot])

    @pl.when(pl.program_id(0) == 0)
    def _():
        at = 0
        for slot, kind in enumerate(kinds):
            if kind == 1:
                copy(refs[at], slot).start()
            else:

                @pl.when(which[0] == 1)
                def _(at=at, slot=slot):
                    copy(refs[at], slot).start()

                @pl.when(which[0] != 1)
                def _(at=at, slot=slot):
                    copy(refs[at + 1], slot).start()

            at += kind
        for slot in range(slots):
            copy(refs[0], slot).wait()

    out_ref[...] = jnp.dot(
        high_ref[...], held[...], preferred_element_type=jnp.float32
    ) + jnp.dot(low_ref[...], held[...], preferred_element_type=jnp.float32)


def product(which, high, low, slots, result, chunk, total_columns):
    rows, depth = high.shape
    kinds = tuple(len(slot) for slot in slots)
    pieces = [piece for slot in slots for piece in slot]
    width = pieces[0].shape[1]
    block = min(ROW_BLOCK, rows)
    given = [] if result is None else [result]
    return pl.pallas_call(
        functools.partial(product_kernel, kinds),
        out_shape=jax.ShapeDtypeStruct((rows, total_columns), jnp.float32),
        grid_spec=pltpu.PrefetchScalarGridSpec(
            num_scalar_prefetch=1,
            grid=(rows // block,),
            in_specs=[pl.BlockSpec((block, depth), lambda i, s: (i, 0))] * 2
            + [pl.BlockSpec(memory_space=pl.ANY)] * (len(pieces) + len(given)),
            out_specs=pl.BlockSpec((block, width), lambda i, s: (i, chunk)),
            scratch_shapes=[
                pltpu.VMEM((depth, width), jnp.bfloat16),
                pltpu.SemaphoreType.DMA((len(slots),)),
            ],
        ),
        input_output_aliases={3 + len(pieces): 0} if given else {},
        cost_estimate=pl.CostEstimate(
            flops=4 * rows * depth * width,
            bytes_accessed=4 * rows * depth + 2 * depth * width + 4 * rows * width,
            transcendentals=0,
        ),
        name="product",
    )(which, high, low, *pieces, *given)


def exchange(right, chunks):
    entries, values, columns = right.shape
    width = columns // chunks
    row_depth = ("row", "depth")
    pairs = [(0, 1), (1, 0), (2, 3), (3, 2)]
    inner = [(1, 2), (2, 1)]
    outward = [(1, 0), (2, 3)]
    swap = [(0, 1), (1, 0)]
    outer_swap = [(0, 1), (1, 0), (6, 7), (7, 6)]
    inner_swap = [(2, 3), (3, 2), (4, 5), (5, 4)]

    def each(arrays, axis, perm):
        return [lax.ppermute(array, axis, perm) for array in arrays]

    own = [
        right[:, :, c * width : (c + 1) * width].reshape(entries * values, width)
        for c in range(chunks)
    ]
    y1 = each(own, "depth", swap)
    p1a = each(own, "row", pairs)
    p1b = each(own, "row", inner)
    y2 = each(p1a, "depth", swap)
    q2a = each(p1b, "row", outward)
    q2b = each(p1a, "row", inner)
    q3 = each(q2b, "row", outward)
    y3a = each(q2a, row_depth, outer_swap)
    y3b = each(q2b, row_depth, inner_swap)
    q3b = each(y1, "row", inner)
    half = chunks // 2
    last = each(q3[:half], row_depth, outer_swap) + each(y3b[half:], "row", outward)
    return [
        [
            (own[c],),
            (p1a[c],),
            (q2a[c], q2b[c]),
            (q3[c], p1b[c]),
            (y1[c],),
            (y2[c],),
            (y3a[c], y3b[c]),
            (last[c], q3b[c]),
        ]
        for c in range(chunks)
    ]


def per_device(shape, left_block, right_block, slice_ids, mode_order):
    rows, depths, cols = shape["row"], shape["depth"], shape["col"]
    entries, values, columns = right_block.shape
    row, depth, col = (lax.axis_index(axis) for axis in ("row", "depth", "col"))
    if (rows, depths) == (4, 2):
        chunks = CHUNKS
        slots = exchange(right_block, chunks)
        sources = jnp.stack(
            [(row ^ s) * depths + (depth ^ t) for t in range(2) for s in range(4)]
        )
    else:
        chunks = 1
        whole = lax.all_gather(
            right_block.reshape(entries * values, columns),
            ("row", "depth"),
            axis=0,
            tiled=True,
        )
        slots = [[(whole,)]]
        sources = jnp.arange(rows * depths, dtype=jnp.int32)
    logical = (
        sources.astype(jnp.int32)[:, None] * entries + jnp.arange(entries, dtype=jnp.int32)[None]
    ).reshape(-1)
    stored = jnp.repeat(stored_order(mode_order, logical), values)
    choice = jnp.tile(jnp.arange(values, dtype=jnp.int32), logical.shape[0])

    if cols == 4:
        across = lax.ppermute(left_block, "col", [(i, i ^ 2) for i in range(4)])
        beside = lax.ppermute(left_block, "col", [(i, i ^ 1) for i in range(4)])
        pieces = [left_block, beside, across]
        pieces.append(lax.ppermute(across, "col", [(i, i ^ 1) for i in range(4)]))
        holders = jnp.stack([col, col ^ 1, col ^ 2, col ^ 3])
    else:
        gathered = lax.all_gather(left_block, "col", axis=0)
        pieces = [gathered[i] for i in range(cols)]
        holders = jnp.arange(cols, dtype=jnp.int32)
    bases = holders.astype(jnp.int32) * left_block.shape[2]

    high, low = fold(pieces, stored, choice, slice_ids, bases)
    which = ((row == 0) | (row == rows - 1)).astype(jnp.int32)[None]
    result = None
    for chunk in range(chunks):
        result = product(which, high, low, slots[chunk], result, chunk, columns)
    return result


def solution(mesh):
    in_specs = (P(None, ("row", "depth"), "col"), P(("row", "depth"), None, "col"), P(), P())
    out_specs = P(("row", "depth"), "col")
    return jax.shard_map(
        functools.partial(per_device, dict(mesh.shape)),
        mesh=mesh,
        in_specs=in_specs,
        out_specs=out_specs,
        check_vma=False,
    )
```
